32 devices in a mesh: corpus: 4 (over y, x), fsdp: 8 (over z, core).
Axes of the slice: x: 2, y: 2, z: 4, core: 2. Of those that a mesh axis runs over, the one named last changes fastest.
Arguments:
- inputs: bfloat16 [2048, 4096], P('fsdp', 'corpus'), may hold values from -128 to 128
- norm_gain: float32 [4096], replicated, may hold values from 0.1 to 1.9
- w_query: bfloat16 [4096, 8192], P('fsdp', 'corpus'), may hold values from -0.09375 to 0.09375
- w_key: bfloat16 [4096, 1024], P('fsdp', 'corpus'), may hold values from -0.09375 to 0.09375
- w_value: bfloat16 [4096, 1024], P('fsdp', 'corpus'), may hold values from -0.375 to 0.375
- query_bias: float32 [8192], P('corpus'), may hold values from -16 to 16
- key_bias: float32 [1024], P('corpus'), may hold values from -16 to 16
- value_bias: float32 [1024], P('corpus'), may hold values from -4 to 4
- key_cache: bfloat16 [8, 2048, 1024], P('fsdp', None, 'corpus'), may hold values from -16 to 16
- value_cache: bfloat16 [8, 2048, 1024], P('fsdp', None, 'corpus'), may hold values from -16 to 16
- source_doc: int32 [32], P('fsdp'), may hold values from 0 to 7, as said below
- prefix_len: int32 [32], P('fsdp'), may hold values from 1 to 2048
Outputs:
- attention: bfloat16 [2048, 8192], P('fsdp', 'corpus')
The draws below stay inside these ranges and needn't reach their ends.
Inputs may be any that keep to these rules, and one draw needn't show every extreme that they name: `source_doc`: within the suffixes of one index of fsdp (aligned blocks of 4) no document appears more than 2 times, and one document, drawn from the seed, appears exactly 2 times in every such block.
All inputs are finite; a program needn't handle non-finite values.
Results may differ from the reference program's by a relative error of at most 0.0075.
The reference program's roundings to bfloat16 on the way (of `normed`, `own_values`, `queries`, `own_keys` and `prefix_normed`) count: a program that leaves them out, or rounds other values in their place, can miss the bound.
Values may be sent and summed in bfloat16 or wider, within the bound.
A program may use at most 128 MiB of HBM per device.

```python
import jax
import jax.numpy as jnp
from jax import lax

D = 4096
HQ = 64
KVH = 8
HD = 128
SL = 64
DOCLEN = 2048
CAP = 2
SUF_DEV = 4
SUFFIXES = 32
TOKENS = 2048
DOCS = 8


def draw_inputs(key, part):
    row_scale = 10.0 ** jax.random.uniform(jax.random.fold_in(key, 1), (TOKENS, 1), jnp.float32, 0.0, 1.0)
    column_scale = 10.0 ** jax.random.uniform(jax.random.fold_in(key, 2), (1, D), jnp.float32, -0.5, 0.5)
    base = jnp.clip(jax.random.normal(jax.random.fold_in(key, 3), (TOKENS, D), jnp.float32), -4.0, 4.0)
    return (base * row_scale * column_scale).astype(jnp.bfloat16)


def draw_query_bias(key, part):
    noise = jnp.clip(0.5 * jax.random.normal(jax.random.fold_in(key, 11), (HQ, HD), jnp.float32), -3.0, 3.0)
    return noise.reshape(HQ * HD)


def draw_key_bias(key, part):
    noise = jnp.clip(0.5 * jax.random.normal(jax.random.fold_in(key, 12), (KVH, HD), jnp.float32), -3.0, 3.0)
    return noise.reshape(KVH * HD)


def draw_key_cache(key, part):
    shape = (DOCS, DOCLEN, KVH, HD)
    base = jnp.clip(jax.random.normal(jax.random.fold_in(key, 21), shape, jnp.float32), -6.0, 6.0)
    return base.reshape(DOCS, DOCLEN, KVH * HD).astype(jnp.bfloat16)


def draw_source_doc(key, part):
    readers = SUFFIXES // SUF_DEV
    favored = jax.random.randint(jax.random.fold_in(key, 5), (), 0, DOCS)

    def one_reader(index):
        local_key = jax.random.fold_in(key, 1000 + index)
        others = jnp.arange((DOCS - 1) * CAP, dtype=jnp.int32) // CAP
        others = others + (others >= favored).astype(jnp.int32)
        mixed = jax.random.permutation(jax.random.fold_in(local_key, 1), others)
        picks = jnp.concatenate([jnp.full((CAP,), favored, jnp.int32), mixed[:SUF_DEV - CAP]])
        return jax.random.permutation(jax.random.fold_in(local_key, 2), picks)
    return jax.vmap(one_reader)(jnp.arange(readers, dtype=jnp.int32)).reshape(SUFFIXES)


def touch_ends(array, key, low, top_value):
    index_at = [jax.random.randint(jax.random.fold_in(key, axis), (), 0, length) for axis, length in enumerate(array.shape)]
    main_axis = array.shape.index(max(array.shape))
    neighbour = index_at[:main_axis] + [(index_at[main_axis] + 1) % array.shape[main_axis]] + index_at[main_axis + 1:]
    return array.at[tuple(index_at)].set(low).at[tuple(neighbour)].set(top_value)


def block_levels(own_key, extent, split, least, largest):
    loudness, own = 1.0, jax.random.fold_in(own_key, 6)
    for dim, shards_of in split:
        heights = jnp.exp(jax.random.uniform(jax.random.fold_in(own, dim), (shards_of,), jnp.float32, least / len(split), largest / len(split)))
        loudness = loudness * jnp.repeat(heights, extent[dim] // shards_of).reshape([-1 if axis == dim else 1 for axis in range(len(extent))])
    return loudness


def scatter_about(key, dims, deviation, reach, cuts=(), kind=jnp.bfloat16):
    loudness = block_levels(key, dims, cuts, -0.22, 0.18) if cuts else 1.0
    values = jax.random.normal(key, dims, jnp.float32) * deviation * loudness
    return jnp.minimum(jnp.maximum(values, -reach), reach).astype(kind)


def setup_inputs(seed: int = 0) -> dict:
    seeds = jax.random.split(jax.random.key(seed), 13)
    return {
        "inputs": draw_inputs(jax.random.fold_in(seeds[12], 71), 0),
        "norm_gain": jnp.clip(1.0 + 0.18 * jax.random.normal(seeds[1], (D,), jnp.float32), 0.1, 1.9),
        "w_query": scatter_about(seeds[2], (D, HQ * HD), D ** -0.5, 0.09375, ((0, 8), (1, 4))),
        "w_key": scatter_about(seeds[3], (D, KVH * HD), D ** -0.5, 0.09375, ((0, 8), (1, 4))),
        "w_value": scatter_about(seeds[4], (D, KVH * HD), (D // 16) ** -0.5, 0.375, ((0, 8), (1, 4))),
        "query_bias": draw_query_bias(jax.random.fold_in(seeds[12], 71), 0),
        "key_bias": draw_key_bias(jax.random.fold_in(seeds[12], 71), 0),
        "value_bias": scatter_about(seeds[7], (KVH * HD,), 1.0, 4.0, ((0, 4),), jnp.float32),
        "key_cache": draw_key_cache(jax.random.fold_in(seeds[12], 71), 0),
        "value_cache": scatter_about(seeds[9], (DOCS, DOCLEN, KVH * HD), 4.0, 16.0, ((0, 8), (2, 4))),
        "source_doc": draw_source_doc(jax.random.fold_in(seeds[12], 71), 0),
        "prefix_len": touch_ends(jax.random.randint(seeds[11], (SUFFIXES,), 1, DOCLEN + 1), jax.random.fold_in(seeds[11], 1), 1, DOCLEN).astype(jnp.int32),
    }


EPS = 1e-06
THETA = 1000000.0
MASKED = -1e+30

def rope_tables(position, width):
    half = width // 2
    freq = THETA ** (-(jnp.arange(half, dtype=jnp.float32) * 2.0 / width))
    angle = position.astype(jnp.float32)[..., None] * freq
    angle = jnp.concatenate([angle, angle], axis=-1)
    return (jnp.cos(angle), jnp.sin(angle))

def rotate(vector, cosine, sine):
    half = vector.shape[-1] // 2
    turned = jnp.concatenate([-vector[..., half:], vector[..., :half]], axis=-1)
    return vector * cosine + turned * sine

def normalize(rows, norm_gain):
    wide = rows.astype(jnp.float32)
    spread = lax.optimization_barrier(jnp.mean(wide * wide, axis=-1, keepdims=True))
    return (wide * lax.rsqrt(spread + EPS) * norm_gain).astype(jnp.bfloat16)

def partial_attend(query, keys, values, live):
    count = query.shape[0]
    width = query.shape[2]
    length = keys.shape[0]
    kv_heads = keys.shape[1] // width
    group = query.shape[1] // kv_heads
    grouped = query.reshape(count, kv_heads, group, width).astype(jnp.float32)
    key_rows = keys.reshape(length, kv_heads, width).astype(jnp.float32)
    scores = jnp.einsum('tkgd,lkd->tkgl', grouped, key_rows) * width ** (-0.5)
    scores = jnp.where(live[:, None, None, :], scores, MASKED)
    peak = lax.optimization_barrier(jnp.max(scores, axis=-1))
    weights = jnp.exp(scores - peak[..., None])
    total = lax.optimization_barrier(jnp.sum(weights, axis=-1))
    rounded = weights.astype(jnp.bfloat16).astype(jnp.float32)
    value_rows = values.reshape(length, kv_heads, width).astype(jnp.float32)
    weighted = jnp.einsum('tkgl,lkd->tkgd', rounded, value_rows)
    return (weighted.reshape(count, kv_heads * group * width), peak.reshape(count, kv_heads * group), total.reshape(count, kv_heads * group))

def settle(part):
    weighted, peak, total = part
    shape = peak.shape + (-1,)
    normed = (weighted.reshape(shape) / total[..., None]).reshape(weighted.shape).astype(jnp.bfloat16)
    return (normed, peak + jnp.log(total))

def combine(prefix_normed, prefix_lse, own):
    own_out, own_peak, own_total = own
    top = jnp.maximum(prefix_lse, own_peak)
    scale_first = jnp.exp(prefix_lse - top)
    scale_second = jnp.exp(own_peak - top)
    divisor = scale_first + own_total * scale_second
    shape = own_peak.shape + (-1,)
    mixed = prefix_normed.astype(jnp.float32).reshape(shape) * scale_first[..., None] + own_out.reshape(shape) * scale_second[..., None]
    mixed = mixed / divisor[..., None]
    return mixed.reshape(own_peak.shape[:-1] + (-1,)).astype(jnp.bfloat16)

def reference(inputs, norm_gain, w_query, w_key, w_value, query_bias, key_bias, value_bias, key_cache, value_cache, source_doc, prefix_len):
    blocks = inputs.reshape(SUFFIXES, SL, D)

    def one_suffix(item):
        rows, document, length = item
        normed = normalize(rows, norm_gain)
        query_lin = jnp.dot(normed, w_query, preferred_element_type=jnp.float32) + query_bias
        key_lin = jnp.dot(normed, w_key, preferred_element_type=jnp.float32) + key_bias
        own_values = (jnp.dot(normed, w_value, preferred_element_type=jnp.float32) + value_bias).astype(jnp.bfloat16)
        position = length + jnp.arange(SL, dtype=jnp.int32)
        cosine, sine = rope_tables(position, HD)
        queries = rotate(query_lin.reshape(SL, HQ, HD), cosine[:, None, :], sine[:, None, :]).astype(jnp.bfloat16)
        own_keys = rotate(key_lin.reshape(SL, KVH, HD), cosine[:, None, :], sine[:, None, :]).astype(jnp.bfloat16)
        doc_keys = lax.dynamic_index_in_dim(key_cache, document, 0, keepdims=False)
        doc_values = lax.dynamic_index_in_dim(value_cache, document, 0, keepdims=False)
        prefix_live = jnp.broadcast_to(jnp.arange(DOCLEN, dtype=jnp.int32)[None, :] < length, (SL, DOCLEN))
        causal = jnp.arange(SL, dtype=jnp.int32)[None, :] <= jnp.arange(SL, dtype=jnp.int32)[:, None]
        prefix_normed, prefix_lse = settle(partial_attend(queries, doc_keys, doc_values, prefix_live))
        own_part = partial_attend(queries, own_keys.reshape(SL, KVH * HD), own_values, causal)
        return combine(prefix_normed, prefix_lse, own_part)
    result = lax.map(one_suffix, (blocks, source_doc, prefix_len))
    return result.reshape(TOKENS, HQ * HD)
```

```python
import jax
import jax.numpy as jnp
from jax import lax
from jax.experimental import pallas as pl
from jax.experimental.pallas import tpu as pltpu
from jax.sharding import PartitionSpec as P

HD = 128
SL = 64
EPS = 1e-06
THETA = 1000000.0
MASKED = -1e30
KEY_BLOCK = 512


def rope_tables(position, width):
    half = width // 2
    freq = THETA ** (-(jnp.arange(half, dtype=jnp.float32) * 2.0 / width))
    angle = position.astype(jnp.float32)[..., None] * freq
    cosine, sine = jnp.cos(angle), jnp.sin(angle)
    return (
        jnp.concatenate([cosine, cosine], axis=-1),
        jnp.concatenate([-sine, sine], axis=-1),
    )


def normalize(rows, norm_gain):
    wide = rows.astype(jnp.float32)
    spread = jnp.mean(wide * wide, axis=-1, keepdims=True)
    return (wide * lax.rsqrt(spread + EPS) * norm_gain).astype(jnp.bfloat16)


def rotate(vector, cosine, sine):
    return vector * cosine + pltpu.roll(vector, HD // 2, 1) * sine


def over_lanes(op, array):
    parts = [array[:, at : at + 128] for at in range(0, array.shape[1], 128)]
    while len(parts) > 1:
        parts = [op(a, b) for a, b in zip(parts[::2], parts[1::2])]
    return parts[0]


def attend_kernel(
    doc_ref,
    len_ref,
    q_ref,
    k_ref,
    v_ref,
    qb_ref,
    kb_ref,
    vb_ref,
    cos_ref,
    sin_ref,
    keys_ref,
    values_ref,
    out_ref,
    scores_ref,
    queries_ref,
    peak_ref,
    total_ref,
    acc_ref,
):
    suffix = pl.program_id(0)
    length = len_ref[suffix]
    scale = HD ** (-0.5)
    group = q_ref.shape[1] // HD
    rows = group * SL
    cosine = cos_ref[...]
    sine = sin_ref[...]
    lin = q_ref[...] + qb_ref[...]
    for h in range(group):
        queries_ref[h * SL : (h + 1) * SL, :] = rotate(
            lin[:, h * HD : (h + 1) * HD], cosine, sine
        ).astype(jnp.bfloat16)
    own_keys = rotate(k_ref[...] + kb_ref[...], cosine, sine).astype(jnp.bfloat16)
    own_values = (v_ref[...] + vb_ref[...]).astype(jnp.bfloat16)
    dims = (((1,), (1,)), ((), ()))

    block = KEY_BLOCK
    blocks = lax.div(length + (block - 1), block)
    peak_ref[...] = jnp.full(peak_ref.shape, MASKED, jnp.float32)

    @pl.loop(0, blocks)
    def _(b):
        at = pl.multiple_of(b * block, block)
        scores = lax.dot_general(
            queries_ref[...],
            keys_ref[0, pl.ds(at, block), :],
            dims,
            preferred_element_type=jnp.float32,
        ) * scale
        column = lax.broadcasted_iota(jnp.int32, (1, block), 1) + at
        scores = jnp.where(column < length, scores, MASKED)
        scores_ref[b] = scores
        peak_ref[...] = jnp.maximum(peak_ref[...], over_lanes(jnp.maximum, scores))

    peak = jnp.max(peak_ref[...], axis=1, keepdims=True)
    peak_ref[...] = jnp.broadcast_to(peak, peak_ref.shape)
    total_ref[...] = jnp.zeros_like(total_ref)
    acc_ref[...] = jnp.zeros_like(acc_ref)

    @pl.loop(0, blocks)
    def _(b):
        at = pl.multiple_of(b * block, block)
        weights = jnp.exp(scores_ref[b] - jnp.tile(peak_ref[...], (1, block // 128)))
        total_ref[...] += over_lanes(jnp.add, weights)
        acc_ref[...] += jnp.dot(
            weights.astype(jnp.bfloat16),
            values_ref[0, pl.ds(at, block), :],
            preferred_element_type=jnp.float32,
        )

    total = jnp.sum(total_ref[...], axis=1, keepdims=True)
    prefix_normed = (acc_ref[...] / total).astype(jnp.bfloat16)
    prefix_lse = peak_ref[...][:, :1] + jnp.log(total)

    own = lax.dot_general(
        queries_ref[...], own_keys, dims, preferred_element_type=jnp.float32
    ) * scale
    token = lax.rem(lax.broadcasted_iota(jnp.int32, (rows, SL), 0), SL)
    other = lax.broadcasted_iota(jnp.int32, (rows, SL), 1)
    own = jnp.where(other <= token, own, MASKED)
    own_peak = jnp.max(own, axis=1, keepdims=True)
    own_weights = jnp.exp(own - own_peak)
    own_total = jnp.sum(own_weights, axis=1, keepdims=True)
    own_out = jnp.dot(
        own_weights.astype(jnp.bfloat16), own_values, preferred_element_type=jnp.float32
    )
    top = jnp.maximum(prefix_lse, own_peak)
    first = jnp.exp(prefix_lse - top)
    second = jnp.exp(own_peak - top)
    divisor = first + own_total * second
    mixed = (prefix_normed.astype(jnp.float32) * first + own_out * second) / divisor
    mixed = mixed.astype(jnp.bfloat16)
    for h in range(group):
        out_ref[:, h * HD : (h + 1) * HD] = mixed[h * SL : (h + 1) * SL, :]


def attend(source_doc, prefix_len, q_lin, k_lin, v_lin, q_bias, k_bias, v_bias, cosine, sine, keys, values):
    suffixes = source_doc.shape[0]
    kv_heads = k_lin.shape[1] // HD
    wide = q_lin.shape[1] // kv_heads
    rows = wide // HD * SL
    length = keys.shape[1]
    block = pl.BlockSpec
    per_head = lambda i, g, doc, size: (i, g)
    bias = lambda i, g, doc, size: (0, g)
    table = lambda i, g, doc, size: (i, 0)
    cached = lambda i, g, doc, size: (doc[i], 0, g)
    flops = 4 * suffixes * kv_heads * rows * length * HD
    return pl.pallas_call(
        attend_kernel,
        out_shape=jax.ShapeDtypeStruct(q_lin.shape, jnp.bfloat16),
        grid_spec=pltpu.PrefetchScalarGridSpec(
            num_scalar_prefetch=2,
            grid=(suffixes, kv_heads),
            in_specs=[
                block((SL, wide), per_head),
                block((SL, HD), per_head),
                block((SL, HD), per_head),
                block((1, wide), bias),
                block((1, HD), bias),
                block((1, HD), bias),
                block((SL, HD), table),
                block((SL, HD), table),
                block((1, length, HD), cached),
                block((1, length, HD), cached),
            ],
            out_specs=block((SL, wide), per_head),
            scratch_shapes=[
                pltpu.VMEM((length // KEY_BLOCK, rows, KEY_BLOCK), jnp.float32),
                pltpu.VMEM((rows, HD), jnp.bfloat16),
                pltpu.VMEM((rows, 128), jnp.float32),
                pltpu.VMEM((rows, 128), jnp.float32),
                pltpu.VMEM((rows, HD), jnp.float32),
            ],
        ),
        compiler_params=pltpu.CompilerParams(
            dimension_semantics=("arbitrary", "arbitrary"), vmem_limit_bytes=40 << 20
        ),
        cost_estimate=pl.CostEstimate(
            flops=flops, transcendentals=flops // (4 * HD), bytes_accessed=16 << 20
        ),
    )(source_doc, prefix_len, q_lin, k_lin, v_lin, q_bias[None], k_bias[None], v_bias[None], cosine, sine, keys, values)


def shards(
    inputs,
    norm_gain,
    w_query,
    w_key,
    w_value,
    query_bias,
    key_bias,
    value_bias,
    key_cache,
    value_cache,
    source_doc,
    prefix_len,
):
    full_rows = lax.all_gather(inputs, "corpus", axis=1, tiled=True)
    normed = normalize(full_rows, norm_gain)

    def project(weight):
        whole = lax.all_gather(weight, "fsdp", axis=0, tiled=True)
        return jnp.dot(normed, whole, preferred_element_type=jnp.float32)

    q_lin, k_lin, v_lin = project(w_query), project(w_key), project(w_value)
    keys = lax.all_gather(key_cache, "fsdp", axis=0, tiled=True)
    values = lax.all_gather(value_cache, "fsdp", axis=0, tiled=True)
    position = prefix_len[:, None] + jnp.arange(SL, dtype=jnp.int32)[None, :]
    cosine, sine = rope_tables(position.reshape(-1), HD)
    return attend(
        source_doc, prefix_len, q_lin, k_lin, v_lin, query_bias, key_bias, value_bias, cosine, sine, keys, values
    )


def solution(mesh):
    in_specs = (
        P("fsdp", "corpus"),
        P(),
        P("fsdp", "corpus"),
        P("fsdp", "corpus"),
        P("fsdp", "corpus"),
        P("corpus"),
        P("corpus"),
        P("corpus"),
        P("fsdp", None, "corpus"),
        P("fsdp", None, "corpus"),
        P("fsdp"),
        P("fsdp"),
    )
    out_specs = P("fsdp", "corpus")
    return jax.shard_map(shards, mesh=mesh, in_specs=in_specs, out_specs=out_specs, check_vma=False)
```

```python
import jax
import jax.numpy as jnp
from jax import lax
from jax.experimental import pallas as pl
from jax.experimental.pallas import tpu as pltpu
from jax.sharding import PartitionSpec as P

HD = 128
SL = 64
EPS = 1e-06
THETA = 1000000.0
MASKED = -1e30
KEY_BLOCK = 512
SENT = jnp.float32


def rope_tables(position, width):
    half = width // 2
    freq = THETA ** (-(jnp.arange(half, dtype=jnp.float32) * 2.0 / width))
    angle = position.astype(jnp.float32)[..., None] * freq
    cosine, sine = jnp.cos(angle), jnp.sin(angle)
    return (
        jnp.concatenate([cosine, cosine], axis=-1),
        jnp.concatenate([-sine, sine], axis=-1),
    )


def normalize(rows, norm_gain):
    wide = rows.astype(jnp.float32)
    spread = jnp.mean(wide * wide, axis=-1, keepdims=True)
    return (wide * lax.rsqrt(spread + EPS) * norm_gain).astype(jnp.bfloat16)


def rotate(vector, cosine, sine):
    return vector * cosine + pltpu.roll(vector, HD // 2, 1) * sine


def over_lanes(op, array):
    parts = [array[:, at : at + 128] for at in range(0, array.shape[1], 128)]
    while len(parts) > 1:
        parts = [op(a, b) for a, b in zip(parts[::2], parts[1::2])]
    return parts[0]


def attend_kernel(
    doc_ref,
    len_ref,
    q_ref,
    k_ref,
    v_ref,
    qb_ref,
    kb_ref,
    vb_ref,
    cos_ref,
    sin_ref,
    keys_ref,
    values_ref,
    out_ref,
    scores_ref,
    queries_ref,
    peak_ref,
    total_ref,
    acc_ref,
):
    suffix = pl.program_id(0)
    length = len_ref[suffix]
    scale = HD ** (-0.5)
    group = q_ref.shape[1] // HD
    rows = group * SL
    cosine = cos_ref[...]
    sine = sin_ref[...]
    lin = q_ref[...] + qb_ref[...]
    for h in range(group):
        queries_ref[h * SL : (h + 1) * SL, :] = rotate(
            lin[:, h * HD : (h + 1) * HD], cosine, sine
        ).astype(jnp.bfloat16)
    own_keys = rotate(k_ref[...] + kb_ref[...], cosine, sine).astype(jnp.bfloat16)
    own_values = (v_ref[...] + vb_ref[...]).astype(jnp.bfloat16)
    dims = (((1,), (1,)), ((), ()))

    block = KEY_BLOCK
    blocks = lax.div(length + (block - 1), block)
    peak_ref[...] = jnp.full(peak_ref.shape, MASKED, jnp.float32)

    @pl.loop(0, blocks)
    def _(b):
        at = pl.multiple_of(b * block, block)
        scores = lax.dot_general(
            queries_ref[...],
            keys_ref[0, pl.ds(at, block), :],
            dims,
            preferred_element_type=jnp.float32,
        ) * scale
        column = lax.broadcasted_iota(jnp.int32, (1, block), 1) + at
        scores = jnp.where(column < length, scores, MASKED)
        scores_ref[b] = scores
        peak_ref[...] = jnp.maximum(peak_ref[...], over_lanes(jnp.maximum, scores))

    peak = jnp.max(peak_ref[...], axis=1, keepdims=True)
    peak_ref[...] = jnp.broadcast_to(peak, peak_ref.shape)
    total_ref[...] = jnp.zeros_like(total_ref)
    acc_ref[...] = jnp.zeros_like(acc_ref)

    @pl.loop(0, blocks)
    def _(b):
        at = pl.multiple_of(b * block, block)
        weights = jnp.exp(scores_ref[b] - jnp.tile(peak_ref[...], (1, block // 128)))
        total_ref[...] += over_lanes(jnp.add, weights)
        acc_ref[...] += jnp.dot(
            weights.astype(jnp.bfloat16),
            values_ref[0, pl.ds(at, block), :],
            preferred_element_type=jnp.float32,
        )

    total = jnp.sum(total_ref[...], axis=1, keepdims=True)
    prefix_normed = (acc_ref[...] / total).astype(jnp.bfloat16)
    prefix_lse = peak_ref[...][:, :1] + jnp.log(total)

    own = lax.dot_general(
        queries_ref[...], own_keys, dims, preferred_element_type=jnp.float32
    ) * scale
    token = lax.rem(lax.broadcasted_iota(jnp.int32, (rows, SL), 0), SL)
    other = lax.broadcasted_iota(jnp.int32, (rows, SL), 1)
    own = jnp.where(other <= token, own, MASKED)
    own_peak = jnp.max(own, axis=1, keepdims=True)
    own_weights = jnp.exp(own - own_peak)
    own_total = jnp.sum(own_weights, axis=1, keepdims=True)
    own_out = jnp.dot(
        own_weights.astype(jnp.bfloat16), own_values, preferred_element_type=jnp.float32
    )
    top = jnp.maximum(prefix_lse, own_peak)
    first = jnp.exp(prefix_lse - top)
    second = jnp.exp(own_peak - top)
    divisor = first + own_total * second
    mixed = (prefix_normed.astype(jnp.float32) * first + own_out * second) / divisor
    mixed = mixed.astype(jnp.bfloat16)
    for h in range(group):
        out_ref[:, h * HD : (h + 1) * HD] = mixed[h * SL : (h + 1) * SL, :]


def attend(source_doc, prefix_len, q_lin, k_lin, v_lin, q_bias, k_bias, v_bias, cosine, sine, keys, values):
    suffixes = source_doc.shape[0]
    kv_heads = k_lin.shape[1] // HD
    wide = q_lin.shape[1] // kv_heads
    rows = wide // HD * SL
    length = keys.shape[1]
    block = pl.BlockSpec
    per_head = lambda i, g, doc, size: (i, g)
    bias = lambda i, g, doc, size: (0, g)
    table = lambda i, g, doc, size: (i, 0)
    cached = lambda i, g, doc, size: (doc[i], 0, g)
    flops = 4 * suffixes * kv_heads * rows * length * HD
    return pl.pallas_call(
        attend_kernel,
        out_shape=jax.ShapeDtypeStruct(q_lin.shape, jnp.bfloat16),
        grid_spec=pltpu.PrefetchScalarGridSpec(
            num_scalar_prefetch=2,
            grid=(suffixes, kv_heads),
            in_specs=[
                block((SL, wide), per_head),
                block((SL, HD), per_head),
                block((SL, HD), per_head),
                block((1, wide), bias),
                block((1, HD), bias),
                block((1, HD), bias),
                block((SL, HD), table),
                block((SL, HD), table),
                block((1, length, HD), cached),
                block((1, length, HD), cached),
            ],
            out_specs=block((SL, wide), per_head),
            scratch_shapes=[
                pltpu.VMEM((length // KEY_BLOCK, rows, KEY_BLOCK), jnp.float32),
                pltpu.VMEM((rows, HD), jnp.bfloat16),
                pltpu.VMEM((rows, 128), jnp.float32),
                pltpu.VMEM((rows, 128), jnp.float32),
                pltpu.VMEM((rows, HD), jnp.float32),
            ],
        ),
        compiler_params=pltpu.CompilerParams(
            dimension_semantics=("arbitrary", "arbitrary"), vmem_limit_bytes=40 << 20
        ),
        cost_estimate=pl.CostEstimate(
            flops=flops, transcendentals=flops // (4 * HD), bytes_accessed=16 << 20
        ),
    )(source_doc, prefix_len, q_lin, k_lin, v_lin, q_bias[None], k_bias[None], v_bias[None], cosine, sine, keys, values)


def gather_all(
    inputs,
    norm_gain,
    w_query,
    w_key,
    w_value,
    query_bias,
    key_bias,
    value_bias,
    key_cache,
    value_cache,
    source_doc,
    prefix_len,
):
    full_rows = lax.all_gather(inputs, "corpus", axis=1, tiled=True)
    normed = normalize(full_rows, norm_gain)

    def project(weight):
        whole = lax.all_gather(weight, "fsdp", axis=0, tiled=True)
        return jnp.dot(normed, whole, preferred_element_type=jnp.float32)

    q_lin, k_lin, v_lin = project(w_query), project(w_key), project(w_value)
    keys = lax.all_gather(key_cache, "fsdp", axis=0, tiled=True)
    values = lax.all_gather(value_cache, "fsdp", axis=0, tiled=True)
    position = prefix_len[:, None] + jnp.arange(SL, dtype=jnp.int32)[None, :]
    cosine, sine = rope_tables(position.reshape(-1), HD)
    return attend(
        source_doc, prefix_len, q_lin, k_lin, v_lin, query_bias, key_bias, value_bias, cosine, sine, keys, values
    )


def swap_cores(array):
    count = lax.axis_size("fsdp")
    return lax.ppermute(array, "fsdp", [(f, f ^ 1) for f in range(count)])


def in_core_order(mine, other, core):
    return jnp.where(core == 0, jnp.stack([mine, other]), jnp.stack([other, mine]))


def half_of(array, which, axis=1):
    size = array.shape[axis] // 2
    return lax.dynamic_slice_in_dim(array, which * size, size, axis)


def along_line(array, step):
    count = lax.axis_size("fsdp")
    held, parts = array, []
    for hop in range(1, count // 2):
        if step > 0:
            sources = range(2 * (hop - 1), count - 2)
        else:
            sources = range(2, count - 2 * (hop - 1))
        held = lax.ppermute(held, "fsdp", [(f, f + 2 * step) for f in sources])
        parts.append(held)
    return parts


def split_heads(
    inputs,
    norm_gain,
    w_query,
    w_key,
    w_value,
    query_bias,
    key_bias,
    value_bias,
    key_cache,
    value_cache,
    source_doc,
    prefix_len,
):
    count = lax.axis_size("fsdp")
    lines = count // 2
    index = lax.axis_index("fsdp")
    core = lax.rem(index, 2)
    line = lax.div(index, 2)
    tokens = inputs.shape[0]

    def cache_table(cache):
        pair = in_core_order(half_of(cache[0], core), swap_cores(half_of(cache[0], 1 - core)), core)
        return jnp.concatenate([pair] + along_line(pair, 1) + along_line(pair, -1))

    keys = cache_table(key_cache)
    values = cache_table(value_cache)

    mine = jnp.concatenate([half_of(w, core) for w in (w_query, w_key, w_value)], axis=1)
    other = swap_cores(
        jnp.concatenate([half_of(w, 1 - core) for w in (w_query, w_key, w_value)], axis=1)
    )
    weight = in_core_order(mine, other, core).reshape(2 * mine.shape[0], mine.shape[1])

    full_rows = lax.all_gather(inputs, "corpus", axis=1, tiled=True)
    normed = normalize(full_rows, norm_gain)
    wide = normed.shape[1] // lines
    by_line = normed.reshape(tokens, lines, wide)
    pieces = [lax.dynamic_index_in_dim(by_line, line, 1, keepdims=False)]
    for shift in range(1, lines):
        sent = lax.dynamic_index_in_dim(by_line, lax.rem(line + shift, lines), 1, keepdims=False)
        pairs = [(f, (f + 2 * shift) % count) for f in range(count)]
        pieces.append(lax.ppermute(sent, "fsdp", pairs))
    block = jnp.stack(pieces)
    both = in_core_order(block, swap_cores(block), core)
    both = jnp.swapaxes(both, 0, 1)
    partial = jnp.einsum("zctd,dn->zctn", both, weight, preferred_element_type=jnp.float32)
    at = lax.rem(line - jnp.arange(lines) + lines, lines)
    partial = jnp.concatenate(
        [lax.dynamic_index_in_dim(partial, at[z], 0) for z in range(lines)]
    ).astype(SENT)
    groups = [[2 * z + c for z in range(lines)] for c in range(2)]
    lin = lax.psum_scatter(
        partial.reshape(count * tokens, -1),
        "fsdp",
        scatter_dimension=0,
        axis_index_groups=groups,
        tiled=True,
    ).astype(jnp.float32)
    heads = query_bias.shape[0] // 2
    q_lin = lin[:, :heads]
    k_lin = lin[:, heads : heads + HD]
    v_lin = lin[:, heads + HD :]

    facts = jnp.stack([source_doc, prefix_len])
    facts = jnp.swapaxes(in_core_order(facts, swap_cores(facts), core), 0, 1).reshape(2, -1)
    docs, lengths = facts[0], facts[1]
    away = line - lax.div(docs, 2)
    slot = 2 * jnp.where(away >= 0, away, lines - 1 - away) + lax.rem(docs, 2)
    position = lengths[:, None] + jnp.arange(SL, dtype=jnp.int32)[None, :]
    cosine, sine = rope_tables(position.reshape(-1), HD)
    out = attend(
        slot,
        lengths,
        q_lin,
        k_lin,
        v_lin,
        half_of(query_bias, core, 0),
        half_of(key_bias, core, 0),
        half_of(value_bias, core, 0),
        cosine,
        sine,
        keys,
        values,
    )
    kept = half_of(out, core, 0)
    got = swap_cores(half_of(out, 1 - core, 0))
    return jnp.where(
        core == 0,
        jnp.concatenate([kept, got], axis=1),
        jnp.concatenate([got, kept], axis=1),
    )


def shards(*arrays):
    lines = lax.axis_size("fsdp") // 2
    if arrays[3].shape[1] == 2 * HD and lines == 4:
        return split_heads(*arrays)
    return gather_all(*arrays)


def solution(mesh):
    in_specs = (
        P("fsdp", "corpus"),
        P(),
        P("fsdp", "corpus"),
        P("fsdp", "corpus"),
        P("fsdp", "corpus"),
        P("corpus"),
        P("corpus"),
        P("corpus"),
        P("fsdp", None, "corpus"),
        P("fsdp", None, "corpus"),
        P("fsdp"),
        P("fsdp"),
    )
    out_specs = P("fsdp", "corpus")
    return jax.shard_map(shards, mesh=mesh, in_specs=in_specs, out_specs=out_specs, check_vma=False)
```

```python
import jax
import jax.numpy as jnp
from jax import lax
from jax.experimental import pallas as pl
from jax.experimental.pallas import tpu as pltpu
from jax.sharding import PartitionSpec as P

HD = 128
SL = 64
EPS = 1e-06
THETA = 1000000.0
MASKED = -1e30
KEY_BLOCK = 512
SENT = jnp.float32


def rope_tables(position, width):
    half = width // 2
    freq = THETA ** (-(jnp.arange(half, dtype=jnp.float32) * 2.0 / width))
    angle = position.astype(jnp.float32)[..., None] * freq
    cosine, sine = jnp.cos(angle), jnp.sin(angle)
    return (
        jnp.concatenate([cosine, cosine], axis=-1),
        jnp.concatenate([-sine, sine], axis=-1),
    )


def normalize(rows, norm_gain):
    wide = rows.astype(jnp.float32)
    spread = jnp.mean(wide * wide, axis=-1, keepdims=True)
    return (wide * lax.rsqrt(spread + EPS) * norm_gain).astype(jnp.bfloat16)


def rotate(vector, cosine, sine):
    return vector * cosine + pltpu.roll(vector, HD // 2, 1) * sine


def over_lanes(op, array):
    parts = [array[:, at : at + 128] for at in range(0, array.shape[1], 128)]
    while len(parts) > 1:
        parts = [op(a, b) for a, b in zip(parts[::2], parts[1::2])]
    return parts[0]


def attend_kernel(
    doc_ref,
    len_ref,
    q_ref,
    k_ref,
    v_ref,
    qb_ref,
    kb_ref,
    vb_ref,
    cos_ref,
    sin_ref,
    keys_ref,
    values_ref,
    out_ref,
    scores_ref,
    queries_ref,
    peak_ref,
    total_ref,
    acc_ref,
):
    suffix = pl.program_id(0)
    length = len_ref[suffix]
    scale = HD ** (-0.5)
    group = q_ref.shape[1] // HD
    rows = group * SL
    cosine = cos_ref[...]
    sine = sin_ref[...]
    lin = q_ref[...] + qb_ref[...]
    for h in range(group):
        queries_ref[h * SL : (h + 1) * SL, :] = rotate(
            lin[:, h * HD : (h + 1) * HD], cosine, sine
        ).astype(jnp.bfloat16)
    own_keys = rotate(k_ref[...] + kb_ref[...], cosine, sine).astype(jnp.bfloat16)
    own_values = (v_ref[...] + vb_ref[...]).astype(jnp.bfloat16)
    dims = (((1,), (1,)), ((), ()))

    block = KEY_BLOCK
    blocks = lax.div(length + (block - 1), block)
    peak_ref[...] = jnp.full(peak_ref.shape, MASKED, jnp.float32)

    @pl.loop(0, blocks)
    def _(b):
        at = pl.multiple_of(b * block, block)
        scores = lax.dot_general(
            queries_ref[...],
            keys_ref[0, pl.ds(at, block), :],
            dims,
            preferred_element_type=jnp.float32,
        ) * scale
        column = lax.broadcasted_iota(jnp.int32, (1, block), 1) + at
        scores = jnp.where(column < length, scores, MASKED)
        scores_ref[b] = scores
        peak_ref[...] = jnp.maximum(peak_ref[...], over_lanes(jnp.maximum, scores))

    peak = jnp.max(peak_ref[...], axis=1, keepdims=True)
    peak_ref[...] = jnp.broadcast_to(peak, peak_ref.shape)
    total_ref[...] = jnp.zeros_like(total_ref)
    acc_ref[...] = jnp.zeros_like(acc_ref)

    @pl.loop(0, blocks)
    def _(b):
        at = pl.multiple_of(b * block, block)
        weights = jnp.exp(scores_ref[b] - jnp.tile(peak_ref[...], (1, block // 128)))
        total_ref[...] += over_lanes(jnp.add, weights)
        acc_ref[...] += jnp.dot(
            weights.astype(jnp.bfloat16),
            values_ref[0, pl.ds(at, block), :],
            preferred_element_type=jnp.float32,
        )

    total = jnp.sum(total_ref[...], axis=1, keepdims=True)
    prefix_normed = (acc_ref[...] / total).astype(jnp.bfloat16)
    prefix_lse = peak_ref[...][:, :1] + jnp.log(total)

    own = lax.dot_general(
        queries_ref[...], own_keys, dims, preferred_element_type=jnp.float32
    ) * scale
    token = lax.rem(lax.broadcasted_iota(jnp.int32, (rows, SL), 0), SL)
    other = lax.broadcasted_iota(jnp.int32, (rows, SL), 1)
    own = jnp.where(other <= token, own, MASKED)
    own_peak = jnp.max(own, axis=1, keepdims=True)
    own_weights = jnp.exp(own - own_peak)
    own_total = jnp.sum(own_weights, axis=1, keepdims=True)
    own_out = jnp.dot(
        own_weights.astype(jnp.bfloat16), own_values, preferred_element_type=jnp.float32
    )
    top = jnp.maximum(prefix_lse, own_peak)
    first = jnp.exp(prefix_lse - top)
    second = jnp.exp(own_peak - top)
    divisor = first + own_total * second
    mixed = (prefix_normed.astype(jnp.float32) * first + own_out * second) / divisor
    mixed = mixed.astype(jnp.bfloat16)
    for h in range(group):
        out_ref[:, h * HD : (h + 1) * HD] = mixed[h * SL : (h + 1) * SL, :]


def attend(source_doc, prefix_len, q_lin, k_lin, v_lin, q_bias, k_bias, v_bias, cosine, sine, keys, values):
    suffixes = source_doc.shape[0]
    kv_heads = k_lin.shape[1] // HD
    wide = q_lin.shape[1] // kv_heads
    rows = wide // HD * SL
    length = keys.shape[1]
    block = pl.BlockSpec
    per_head = lambda i, g, doc, size: (i, g)
    bias = lambda i, g, doc, size: (0, g)
    table = lambda i, g, doc, size: (i, 0)
    cached = lambda i, g, doc, size: (doc[i], 0, g)
    flops = 4 * suffixes * kv_heads * rows * length * HD
    return pl.pallas_call(
        attend_kernel,
        out_shape=jax.ShapeDtypeStruct(q_lin.shape, jnp.bfloat16),
        grid_spec=pltpu.PrefetchScalarGridSpec(
            num_scalar_prefetch=2,
            grid=(suffixes, kv_heads),
            in_specs=[
                block((SL, wide), per_head),
                block((SL, HD), per_head),
                block((SL, HD), per_head),
                block((1, wide), bias),
                block((1, HD), bias),
                block((1, HD), bias),
                block((SL, HD), table),
                block((SL, HD), table),
                block((1, length, HD), cached),
                block((1, length, HD), cached),
            ],
            out_specs=block((SL, wide), per_head),
            scratch_shapes=[
                pltpu.VMEM((length // KEY_BLOCK, rows, KEY_BLOCK), jnp.float32),
                pltpu.VMEM((rows, HD), jnp.bfloat16),
                pltpu.VMEM((rows, 128), jnp.float32),
                pltpu.VMEM((rows, 128), jnp.float32),
                pltpu.VMEM((rows, HD), jnp.float32),
            ],
        ),
        compiler_params=pltpu.CompilerParams(
            dimension_semantics=("arbitrary", "arbitrary"), vmem_limit_bytes=40 << 20
        ),
        cost_estimate=pl.CostEstimate(
            flops=flops, transcendentals=flops // (4 * HD), bytes_accessed=16 << 20
        ),
    )(source_doc, prefix_len, q_lin, k_lin, v_lin, q_bias[None], k_bias[None], v_bias[None], cosine, sine, keys, values)


def gather_all(
    inputs,
    norm_gain,
    w_query,
    w_key,
    w_value,
    query_bias,
    key_bias,
    value_bias,
    key_cache,
    value_cache,
    source_doc,
    prefix_len,
):
    full_rows = lax.all_gather(inputs, "corpus", axis=1, tiled=True)
    normed = normalize(full_rows, norm_gain)

    def project(weight):
        whole = lax.all_gather(weight, "fsdp", axis=0, tiled=True)
        return jnp.dot(normed, whole, preferred_element_type=jnp.float32)

    q_lin, k_lin, v_lin = project(w_query), project(w_key), project(w_value)
    keys = lax.all_gather(key_cache, "fsdp", axis=0, tiled=True)
    values = lax.all_gather(value_cache, "fsdp", axis=0, tiled=True)
    position = prefix_len[:, None] + jnp.arange(SL, dtype=jnp.int32)[None, :]
    cosine, sine = rope_tables(position.reshape(-1), HD)
    return attend(
        source_doc, prefix_len, q_lin, k_lin, v_lin, query_bias, key_bias, value_bias, cosine, sine, keys, values
    )


def swap_cores(array):
    count = lax.axis_size("fsdp")
    return lax.ppermute(array, "fsdp", [(f, f ^ 1) for f in range(count)])


def in_core_order(mine, other, core):
    return jnp.where(core == 0, jnp.stack([mine, other]), jnp.stack([other, mine]))


def half_of(array, which, axis=1):
    size = array.shape[axis] // 2
    return lax.dynamic_slice_in_dim(array, which * size, size, axis)


def one_hop(array, hop, step):
    count = lax.axis_size("fsdp")
    if step > 0:
        sources = range(2 * (hop - 1), count - 2)
    else:
        sources = range(2, count - 2 * (hop - 1))
    return lax.ppermute(array, "fsdp", [(f, f + 2 * step) for f in sources])


def hop_both(held, hop):
    return [one_hop(array, hop, step) for array, step in zip(held, (1, -1, 1, -1))]


def split_heads(
    inputs,
    norm_gain,
    w_query,
    w_key,
    w_value,
    query_bias,
    key_bias,
    value_bias,
    key_cache,
    value_cache,
    source_doc,
    prefix_len,
):
    count = lax.axis_size("fsdp")
    lines = count // 2
    index = lax.axis_index("fsdp")
    core = lax.rem(index, 2)
    line = lax.div(index, 2)
    tokens = inputs.shape[0]

    def pair_of(cache):
        return in_core_order(half_of(cache[0], core), swap_cores(half_of(cache[0], 1 - core)), core)

    own_k, own_v = pair_of(key_cache), pair_of(value_cache)
    hop1 = hop_both([own_k, own_k, own_v, own_v], 1)

    mine = jnp.concatenate([half_of(w, core) for w in (w_query, w_key, w_value)], axis=1)
    other = swap_cores(
        jnp.concatenate([half_of(w, 1 - core) for w in (w_query, w_key, w_value)], axis=1)
    )
    weight = in_core_order(mine, other, core).reshape(2 * mine.shape[0], mine.shape[1])

    full_rows = lax.all_gather(inputs, "corpus", axis=1, tiled=True)
    normed = normalize(full_rows, norm_gain)
    normed, weight, hop1 = lax.optimization_barrier((normed, weight, hop1))
    hop2 = hop_both(hop1, 2)
    wide = normed.shape[1] // lines
    by_line = normed.reshape(tokens, lines, wide)
    pieces = [lax.dynamic_index_in_dim(by_line, line, 1, keepdims=False)]
    for shift in range(1, lines):
        sent = lax.dynamic_index_in_dim(by_line, lax.rem(line + shift, lines), 1, keepdims=False)
        pairs = [(f, (f + 2 * shift) % count) for f in range(count)]
        pieces.append(lax.ppermute(sent, "fsdp", pairs))
    block = jnp.stack(pieces)
    both = in_core_order(block, swap_cores(block), core)
    both = jnp.swapaxes(both, 0, 1)
    at = lax.rem(line - jnp.arange(lines) + lines, lines)
    both = jnp.concatenate([lax.dynamic_index_in_dim(both, at[z], 0) for z in range(lines)])
    both, hop2 = lax.optimization_barrier((both.reshape(count * tokens, -1), hop2))
    hop3 = hop_both(hop2, 3)
    partial = jnp.dot(both, weight, preferred_element_type=jnp.float32).astype(SENT)
    groups = [[2 * z + c for z in range(lines)] for c in range(2)]
    lin = lax.psum_scatter(
        partial,
        "fsdp",
        scatter_dimension=0,
        axis_index_groups=groups,
        tiled=True,
    ).astype(jnp.float32)
    keys = jnp.concatenate([own_k] + [hop[i] for i in (0, 1) for hop in (hop1, hop2, hop3)])
    values = jnp.concatenate([own_v] + [hop[i] for i in (2, 3) for hop in (hop1, hop2, hop3)])
    heads = query_bias.shape[0] // 2
    q_lin = lin[:, :heads]
    k_lin = lin[:, heads : heads + HD]
    v_lin = lin[:, heads + HD :]

    facts = jnp.stack([source_doc, prefix_len])
    facts = jnp.swapaxes(in_core_order(facts, swap_cores(facts), core), 0, 1).reshape(2, -1)
    docs, lengths = facts[0], facts[1]
    away = line - lax.div(docs, 2)
    slot = 2 * jnp.where(away >= 0, away, lines - 1 - away) + lax.rem(docs, 2)
    position = lengths[:, None] + jnp.arange(SL, dtype=jnp.int32)[None, :]
    cosine, sine = rope_tables(position.reshape(-1), HD)
    out = attend(
        slot,
        lengths,
        q_lin,
        k_lin,
        v_lin,
        half_of(query_bias, core, 0),
        half_of(key_bias, core, 0),
        half_of(value_bias, core, 0),
        cosine,
        sine,
        keys,
        values,
    )
    kept = half_of(out, core, 0)
    got = swap_cores(half_of(out, 1 - core, 0))
    return jnp.where(
        core == 0,
        jnp.concatenate([kept, got], axis=1),
        jnp.concatenate([got, kept], axis=1),
    )


def shards(*arrays):
    lines = lax.axis_size("fsdp") // 2
    if arrays[3].shape[1] == 2 * HD and lines == 4:
        return split_heads(*arrays)
    return gather_all(*arrays)


def solution(mesh):
    in_specs = (
        P("fsdp", "corpus"),
        P(),
        P("fsdp", "corpus"),
        P("fsdp", "corpus"),
        P("fsdp", "corpus"),
        P("corpus"),
        P("corpus"),
        P("corpus"),
        P("fsdp", None, "corpus"),
        P("fsdp", None, "corpus"),
        P("fsdp"),
        P("fsdp"),
    )
    out_specs = P("fsdp", "corpus")
    return jax.shard_map(shards, mesh=mesh, in_specs=in_specs, out_specs=out_specs, check_vma=False)
```
